32 devices in a mesh: blk: 16 (over z, y, core), rel: 2 (over x).
Axes of the slice: x: 2, y: 2, z: 4, core: 2. Of those that a mesh axis runs over, the one named last changes fastest.
Arguments:
- user_table: float32 [16384, 512], P(('blk', 'rel')), may hold values from -1.5 to 1.5
- user_accum: float32 [16384], P(('blk', 'rel')), may hold values from 1 to 100
- item_table: float32 [32768, 512], P(('blk', 'rel')), may hold values from -1.5 to 1.5
- item_accum: float32 [32768], P(('blk', 'rel')), may hold values from 1 to 100
- relation: bfloat16 [512, 512], replicated, may hold values from -0.25 to 0.25
- relation_accum: float32 [512], replicated, may hold values from 0.5 to 8
- targets: bfloat16 [2, 16384, 2048], P(None, 'blk', 'rel'), may hold values from 0 to 1
Outputs:
- user_table_next: float32 [16384, 512], P(('blk', 'rel'))
- user_accum_next: float32 [16384], P(('blk', 'rel'))
- item_table_next: float32 [32768, 512], P(('blk', 'rel'))
- item_accum_next: float32 [32768], P(('blk', 'rel'))
- relation_step: float32 [512, 512], replicated
- relation_accum_next: float32 [512], replicated
The draws below stay inside these ranges and needn't reach their ends.
All inputs are finite; a program needn't handle non-finite values.
Results may differ from the reference program's by a relative error of at most 0.0037.
The reference program's roundings to bfloat16 on the way count: a program that leaves them out, or rounds other values in their place, can miss the bound.
Values may be sent and summed in bfloat16 or wider, within the bound.
No kernel may reach another device: no remote copies, remote signals or barrier semaphores. Data moves between devices by JAX's collectives and lax.ppermute only.
A program may use at most 64 MiB of HBM per device.

```python
import math
import jax
import jax.numpy as jnp
from jax import lax

D = 512
U_ROWS = 1024
I_ROWS = 2048
ROUNDS = 2
NB = 16
NU = 16384
NI = 32768


def levels(stream_key, dims, cuts, low, top_value):
    def one(dim, blocks):
        draws = jax.random.uniform(jax.random.fold_in(jax.random.fold_in(stream_key, 6), dim), (blocks,), jnp.float32, low / len(cuts), top_value / len(cuts))
        return jnp.repeat(jnp.exp(draws), dims[dim] // blocks).reshape((-1,) + (1,) * (len(dims) - dim - 1))

    level = one(*cuts[0])
    for cut in cuts[1:]:
        level = level * one(*cut)
    return level


def normal_values(stream_key, dims, spread, most, cuts=(), dtype=jnp.bfloat16):
    loudness = levels(stream_key, dims, cuts, -0.22, 0.18) if cuts else 1.0
    entries = jax.random.normal(stream_key, dims, jnp.float32) * spread * loudness
    return jnp.minimum(jnp.maximum(entries, -most), most).astype(dtype)


def setup_inputs(seed: int = 0) -> dict:
    key_list = jax.random.split(jax.random.key(seed), 8)
    user_table = normal_values(key_list[0], (NU, D), 0.25, 1.5, ((0, 32),), jnp.float32)
    user_accum = jnp.clip(jnp.exp(math.log(100.0) - 4.6051702 * jax.random.uniform(key_list[1], (NU,), jnp.float32) ** levels(key_list[1], (NU,), ((0, 32),), -0.2, 0.2)), 1.0, 100.0)
    item_table = normal_values(key_list[2], (NI, D), 0.25, 1.5, ((0, 32),), jnp.float32)
    item_accum = jnp.clip(jnp.exp(math.log(100.0) - 4.6051702 * jax.random.uniform(key_list[3], (NI,), jnp.float32) ** levels(key_list[3], (NI,), ((0, 32),), -0.2, 0.2)), 1.0, 100.0)
    relation = normal_values(key_list[4], (D, D), D ** -0.5, 0.25)
    relation_accum = jnp.clip(jnp.exp(jax.random.uniform(key_list[5], (D,), jnp.float32, math.log(0.5), math.log(8.0))), 0.5, 8.0)
    targets = jnp.clip(1.0 * jax.random.uniform(key_list[6], (ROUNDS, NU, I_ROWS), jnp.float32) ** levels(key_list[6], (ROUNDS, NU, I_ROWS), ((1, 16), (2, 2)), -0.2, 0.2), 0.0, 1.0).astype(jnp.bfloat16)
    return dict(user_table=user_table, user_accum=user_accum, item_table=item_table, item_accum=item_accum, relation=relation, relation_accum=relation_accum, targets=targets)


learn_rate = 0.1
epsilon = 1e-06

def adagrad_rows(table, accum, grads):
    accum_next = accum + lax.optimization_barrier(jnp.mean(grads * grads, axis=1))
    return (table - learn_rate * grads * lax.rsqrt(accum_next + epsilon)[:, None], accum_next)

def reference(user_table, user_accum, item_table, item_accum, relation, relation_accum, targets):
    user_parts = user_table.reshape(NB, U_ROWS, D)
    user_sums = user_accum.reshape(NB, U_ROWS)
    item_parts = item_table.reshape(NB, I_ROWS, D)
    item_sums = item_accum.reshape(NB, I_ROWS)
    label_parts = targets.reshape(ROUNDS, NB, U_ROWS, I_ROWS)
    total = jnp.zeros((D, D), jnp.float32)

    def bucket(carry, inputs):
        users, uacc, items, iacc, labels_now = inputs
        user_bf = users.astype(jnp.bfloat16)
        item_bf = items.astype(jnp.bfloat16)
        anchor = jnp.dot(user_bf, relation, preferred_element_type=jnp.float32).astype(jnp.bfloat16)
        scores = jnp.dot(anchor, item_bf.T, preferred_element_type=jnp.float32)
        errors = (jax.nn.sigmoid(scores) - labels_now.astype(jnp.float32)).astype(jnp.bfloat16)
        mapped = jnp.dot(item_bf, relation.T, preferred_element_type=jnp.float32).astype(jnp.bfloat16)
        user_grad = jnp.dot(errors, mapped, preferred_element_type=jnp.float32)
        item_grad = jnp.dot(errors.T, anchor, preferred_element_type=jnp.float32)
        crossed = jnp.dot(user_bf.T, errors, preferred_element_type=jnp.float32).astype(jnp.bfloat16)
        carry = carry + jnp.dot(crossed, item_bf, preferred_element_type=jnp.float32)
        users_new, uacc_new = adagrad_rows(users, uacc, user_grad)
        items_new, iacc_new = adagrad_rows(items, iacc, item_grad)
        return (carry, (users_new, uacc_new, items_new, iacc_new))
    for turn in range(ROUNDS):
        total, (user_parts, user_sums, item_parts, item_sums) = lax.scan(bucket, total, (user_parts, user_sums, item_parts, item_sums, label_parts[turn]))
        item_parts = jnp.roll(item_parts, 1, axis=0)
        item_sums = jnp.roll(item_sums, 1, axis=0)
    mean_grad = total / (NB * ROUNDS)
    accum_next = relation_accum + lax.optimization_barrier(jnp.mean(mean_grad * mean_grad, axis=1))
    relation_step = mean_grad * lax.rsqrt(accum_next + epsilon)[:, None]
    return (user_parts.reshape(NU, D), user_sums.reshape(NU), item_parts.reshape(NI, D), item_sums.reshape(NI), relation_step, accum_next)
```

```python
import jax
import jax.numpy as jnp
from jax import lax
from jax.sharding import PartitionSpec as P

learn_rate = 0.1
epsilon = 1e-06
narrow = jnp.bfloat16


def exchange(x, flip, rel_flip):
    blocks, rels = lax.axis_size("blk"), lax.axis_size("rel")
    pairs = [
        (b * rels + r, (b ^ flip) * rels + (r ^ rel_flip)) for b in range(blocks) for r in range(rels)
    ]
    return lax.ppermute(x, ("blk", "rel"), pairs)


def swap(x):
    return exchange(x, 0, 1)


def from_behind(x):
    peers = lax.axis_size("blk")
    return lax.ppermute(x, "blk", [(i, (i + 1) % peers) for i in range(peers)])


def wide(x):
    return x.astype(jnp.float32)


def dot(a, b, da, db):
    return lax.dot_general(a, b, (((da,), (db,)), ((), ())), preferred_element_type=jnp.float32)


def adagrad_rows(table, accum, grads):
    accum_next = accum + jnp.mean(grads * grads, axis=1)
    return (table - learn_rate * grads * lax.rsqrt(accum_next + epsilon)[:, None], accum_next)


def pick(parts, key):
    n = len(parts)
    level = 1
    while level < n:
        bit = (key // level) % 2 == 1
        parts = [
            jnp.where(bit, parts[k ^ level], parts[k]) for k in range(n)
        ]
        level *= 2
    return jnp.concatenate(parts, axis=0)


def relation_total(p):
    blocks = lax.axis_size("blk")
    b, r = lax.axis_index("blk"), lax.axis_index("rel")
    core = b % 2
    with jax.named_scope("rel_core"):
        half = p.shape[0] // 2
        mine = lax.dynamic_slice_in_dim(p, core * half, half)
        other = lax.dynamic_slice_in_dim(p, (1 - core) * half, half)
        p = mine + exchange(other, 1, 0)
    with jax.named_scope("rel_xy"):
        key = r + 2 * ((b // 2) % 2)
        part = half // 4
        total = lax.dynamic_slice_in_dim(p, key * part, part)
        got = []
        for k in (3, 1, 2):
            piece = lax.dynamic_slice_in_dim(p, (key ^ k) * part, part).astype(narrow)
            got.append(wide(exchange(piece, 2 * (k // 2), k % 2)))
        total = total + (got[0] + (got[1] + got[2]))
    with jax.named_scope("rel_z"):
        flip = 4
        while blocks // flip > 8:
            sent = total.astype(narrow)
            total = wide(sent) + wide(exchange(sent, flip, 0))
            flip *= 2
        sent = total.astype(narrow)
        parts = [wide(sent)] + [wide(exchange(sent, flip * k, 0)) for k in range(1, blocks // flip)]
        while len(parts) > 1:
            parts = [parts[i] + parts[i + 1] for i in range(0, len(parts), 2)]
        sent = parts[0].astype(narrow)
    with jax.named_scope("rel_xy_back"):
        parts = [sent] + [exchange(sent, 2 * (k // 2), k % 2) for k in (1, 2, 3)]
        p = pick(parts, key)
    with jax.named_scope("rel_core_back"):
        return pick([p, exchange(p, 1, 0)], core)


def per_device(user_table, user_accum, item_table, item_accum, relation, relation_accum, targets):
    blocks = lax.axis_size("blk")
    rounds = targets.shape[0]
    rows = user_table.shape[0]
    r = lax.axis_index("rel")

    mine, theirs = user_table.astype(narrow), None
    theirs = swap(mine)
    mine_f, theirs_f = user_table, None
    mine_acc, theirs_acc = user_accum, swap(user_accum)
    items, item_sums = item_table, item_accum
    relation_local = None
    for turn in range(rounds):
        last = turn == rounds - 1
        item_bf = items.astype(narrow)
        labels = [
            lax.dynamic_slice_in_dim(targets[turn], which * rows, rows) for which in (r, 1 - r)
        ]
        mapped = dot(item_bf, relation, 1, 1).astype(narrow)

        def errors_of(users, label):
            anchor = dot(users, relation, 1, 0).astype(narrow)
            scores = dot(anchor, item_bf, 1, 1)
            return anchor, (jax.nn.sigmoid(scores) - wide(label)).astype(narrow)

        with jax.named_scope(f"own_{turn}"):
            anchor_o, errors_o = errors_of(mine, labels[0])
            grad_o = dot(errors_o, mapped, 1, 0)
            if not last:
                grad_o_there = swap(grad_o.astype(narrow))
        with jax.named_scope(f"peer_{turn}"):
            anchor_p, errors_p = errors_of(theirs, labels[1])
            grad_p = dot(errors_p, mapped, 1, 0)
            grad_o = grad_o + wide(swap(grad_p.astype(narrow)))
        with jax.named_scope(f"items_{turn}"):
            item_grad = dot(errors_o, anchor_o, 0, 0) + dot(errors_p, anchor_p, 0, 0)
            items_next, item_sums = adagrad_rows(wide(items), item_sums, item_grad)
            items_next = from_behind(items_next.astype(narrow))
            item_sums = from_behind(item_sums)
        with jax.named_scope(f"term_{turn}"):
            crossed = (dot(mine, errors_o, 0, 0) + dot(theirs, errors_p, 0, 0)).astype(narrow)
            term = dot(crossed, item_bf, 1, 0)
            relation_local = term if relation_local is None else relation_local + term
        with jax.named_scope(f"users_{turn}"):
            mine_f, mine_acc = adagrad_rows(mine_f, mine_acc, grad_o)
            mine = mine_f.astype(narrow)
            if not last:
                grad_p = grad_p + wide(grad_o_there)
                theirs_f, theirs_acc = adagrad_rows(
                    wide(theirs) if theirs_f is None else theirs_f, theirs_acc, grad_p
                )
                theirs = theirs_f.astype(narrow)
        items = items_next
    total = wide(relation_total(relation_local))
    with jax.named_scope("rel_final"):
        mean_grad = total / (blocks * rounds)
        accum_next = relation_accum + jnp.mean(mean_grad * mean_grad, axis=1)
        relation_step = mean_grad * lax.rsqrt(accum_next + epsilon)[:, None]
    return (mine_f, mine_acc, wide(items), item_sums, relation_step, accum_next)


def solution(mesh):
    rows = P(("blk", "rel"), None)
    line = P(("blk", "rel"))
    return jax.shard_map(
        per_device,
        mesh=mesh,
        in_specs=(rows, line, rows, line, P(), P(), P(None, "blk", "rel")),
        out_specs=(rows, line, rows, line, P(), P()),
        check_vma=False,
    )
```

```python
import functools

import jax
import jax.numpy as jnp
from jax import lax
from jax.experimental import pallas as pl
from jax.experimental.pallas import tpu as pltpu
from jax.sharding import PartitionSpec as P

learn_rate = 0.1
epsilon = 1e-06
narrow = jnp.bfloat16
single = jnp.float32
TILE = 256


def exchange(x, flip, rel_flip):
    blocks, rels = lax.axis_size("blk"), lax.axis_size("rel")
    pairs = [
        (b * rels + r, (b ^ flip) * rels + (r ^ rel_flip)) for b in range(blocks) for r in range(rels)
    ]
    return lax.ppermute(x, ("blk", "rel"), pairs)


def swap(x):
    return exchange(x, 0, 1)


def from_behind(x):
    peers = lax.axis_size("blk")
    return lax.ppermute(x, "blk", [(i, (i + 1) % peers) for i in range(peers)])


def wide(x):
    return x.astype(single)


def dot(a, b, da, db):
    return lax.dot_general(a, b, (((da,), (db,)), ((), ())), preferred_element_type=single)


def as_column(line):
    return jnp.transpose(jnp.broadcast_to(line, (8, line.shape[1])))[:, :1]


def as_line(column):
    return jnp.transpose(jnp.broadcast_to(column, (column.shape[0], 128)))[:1, :]


def adagrad_rows(table, accum, grads):
    accum_next = accum + jnp.sum(grads * grads, axis=1, keepdims=True) * (1.0 / grads.shape[1])
    return table - grads * (learn_rate * lax.rsqrt(accum_next + epsilon)), accum_next


def whole(*shape):
    return pl.BlockSpec(shape, lambda *_: (0,) * len(shape))


def shape(dtype, *dims):
    return jax.ShapeDtypeStruct(dims, dtype)


def call(body, name, grid, in_specs, out_specs, out_shape, scratch, flops, prefetch=0, limit=32):
    return pl.pallas_call(
        body,
        name=name,
        grid_spec=pltpu.PrefetchScalarGridSpec(
            num_scalar_prefetch=prefetch,
            grid=grid,
            in_specs=in_specs,
            out_specs=out_specs,
            scratch_shapes=scratch,
        ),
        out_shape=out_shape,
        compiler_params=pltpu.CompilerParams(
            dimension_semantics=("arbitrary",) * len(grid), vmem_limit_bytes=limit << 20
        ),
        cost_estimate=pl.CostEstimate(flops=flops, bytes_accessed=4 << 20, transcendentals=0),
    )


def errors_of(scores, labels):
    return (jax.nn.sigmoid(scores) - wide(labels)).astype(narrow)


def first_body(place, users, items, relation, labels, items_b, mapped, anchor, errors, grad, grad_b):
    j = pl.program_id(0)

    @pl.when(j == 0)
    def _():
        anchor[...] = dot(users[...], relation[...], 1, 0).astype(narrow)

    block = items[...].astype(narrow)
    items_b[...] = block
    mapped[...] = dot(block, relation[...], 1, 1).astype(narrow)
    found = errors_of(dot(anchor[...], block, 1, 1), labels[...])
    errors[...] = found
    part = dot(found, mapped[...], 1, 0)

    @pl.when(j == 0)
    def _():
        grad[...] = part

    @pl.when(j > 0)
    def _():
        grad[...] += part

    @pl.when(j == pl.num_programs(0) - 1)
    def _():
        grad_b[...] = grad[...].astype(narrow)


def first_own(place, users, items, relation, targets, turn):
    n, d = users.shape
    m = items.shape[0]
    tile = pl.BlockSpec((TILE, d), lambda j, place: (j, 0))
    labels = pl.BlockSpec((None, n, TILE), lambda j, place: (turn, place[0], j))
    return call(
        first_body,
        "first_own",
        (m // TILE,),
        [whole(n, d), tile, whole(d, d), labels],
        [
            tile,
            tile,
            whole(n, d),
            pl.BlockSpec((n, TILE), lambda j, place: (0, j)),
            whole(n, d),
            whole(n, d),
        ],
        [
            shape(narrow, m, d),
            shape(narrow, m, d),
            shape(narrow, n, d),
            shape(narrow, n, m),
            shape(single, n, d),
            shape(narrow, n, d),
        ],
        [],
        2 * n * d * d + 2 * m * d * d + 4 * n * m * d,
        prefetch=1,
    )(place, users, items, relation, targets)


def peer_body(place, users, items, mapped, relation, labels, anchor, errors, grad, grad_b):
    j = pl.program_id(0)

    @pl.when(j == 0)
    def _():
        anchor[...] = dot(users[...], relation[...], 1, 0).astype(narrow)

    found = errors_of(dot(anchor[...], items[...], 1, 1), labels[...])
    errors[...] = found
    part = dot(found, mapped[...], 1, 0)

    @pl.when(j == 0)
    def _():
        grad[...] = part

    @pl.when(j > 0)
    def _():
        grad[...] += part

    @pl.when(j == pl.num_programs(0) - 1)
    def _():
        grad_b[...] = grad[...].astype(narrow)


def first_peer(place, users, items, mapped, relation, targets, turn):
    n, d = users.shape
    m = items.shape[0]
    tile = pl.BlockSpec((TILE, d), lambda j, place: (j, 0))
    labels = pl.BlockSpec((None, n, TILE), lambda j, place: (turn, 1 - place[0], j))
    return call(
        peer_body,
        "first_peer",
        (m // TILE,),
        [whole(n, d), tile, tile, whole(d, d), labels],
        [whole(n, d), pl.BlockSpec((n, TILE), lambda j, place: (0, j)), whole(n, d), whole(n, d)],
        [shape(narrow, n, d), shape(narrow, n, m), shape(single, n, d), shape(narrow, n, d)],
        [],
        2 * n * d * d + 4 * n * m * d,
        prefetch=1,
    )(place, users, items, mapped, relation, targets)


def items_body(errors_o, errors_p, anchor_o, anchor_p, items, sums, items_next, sums_next):
    grads = dot(errors_o[...], anchor_o[...], 0, 0) + dot(errors_p[...], anchor_p[...], 0, 0)
    table, accum = adagrad_rows(wide(items[...]), as_column(sums[...]), grads)
    items_next[...] = table.astype(narrow)
    sums_next[...] = as_line(accum)


def update_items(errors, anchors, items, sums):
    m, d = items.shape
    n = anchors[0][0].shape[0] if anchors[0][0] is not anchors[1][0] else anchors[0][0].shape[0] // 2
    tile = pl.BlockSpec((TILE, d), lambda j: (j, 0))
    line = pl.BlockSpec((1, TILE), lambda j: (0, j))
    return call(
        items_body,
        "update_items",
        (m // TILE,),
        [pl.BlockSpec((n, TILE), lambda j, at=at: (at, j)) for _, at in errors]
        + [pl.BlockSpec((n, d), lambda j, at=at: (at, 0)) for _, at in anchors]
        + [tile, line],
        [tile, line],
        [shape(narrow, m, d), shape(single, 1, m)],
        [],
        4 * n * m * d,
    )(errors[0][0], errors[1][0], anchors[0][0], anchors[1][0], items, sums)


def term_body(users_o, users_p, errors_o, errors_p, items, term, turned_o, turned_p):
    j = pl.program_id(0)

    @pl.when(j == 0)
    def _():
        turned_o[...] = jnp.transpose(users_o[...])
        turned_p[...] = jnp.transpose(users_p[...])

    crossed = dot(turned_o[...], errors_o[...], 1, 0) + dot(turned_p[...], errors_p[...], 1, 0)
    part = dot(crossed.astype(narrow), items[...], 1, 0)

    @pl.when(j == 0)
    def _():
        term[...] = part

    @pl.when(j > 0)
    def _():
        term[...] += part


def first_term(users_o, users_p, errors_o, errors_p, items):
    n, d = users_o.shape
    m = items.shape[0]
    tile = pl.BlockSpec((TILE, d), lambda j: (j, 0))
    side = pl.BlockSpec((n, TILE), lambda j: (0, j))
    return call(
        term_body,
        "first_term",
        (m // TILE,),
        [whole(n, d), whole(n, d), side, side, tile],
        whole(d, d),
        shape(single, d, d),
        [pltpu.VMEM((d, n), narrow), pltpu.VMEM((d, n), narrow)],
        4 * n * m * d + 2 * m * d * d,
    )(users_o, users_p, errors_o, errors_p, items)


def second_body(
    place,
    table_o, table_p, grad_o, grad_p, more_o, more_p, sums_o, sums_p,
    relation, items, labels_o, labels_p, term_before,
    users_next, sums_next, anchor, errors, term,
    turned,
):
    j = pl.program_id(0)
    n = table_o.shape[0]

    @pl.when(j == 0)
    def _():
        table, accum = adagrad_rows(table_o[...], as_column(sums_o[...]), grad_o[...] + wide(more_o[...]))
        users_next[...] = table
        sums_next[...] = as_line(accum)
        own = table.astype(narrow)
        turned[:, :n] = jnp.transpose(own)
        anchor[:n, :] = dot(own, relation[...], 1, 0).astype(narrow)
        table, _ = adagrad_rows(wide(table_p[...]), as_column(sums_p[...]), grad_p[...] + wide(more_p[...]))
        peer = table.astype(narrow)
        turned[:, n:] = jnp.transpose(peer)
        anchor[n:, :] = dot(peer, relation[...], 1, 0).astype(narrow)

    block = items[...]
    scores = dot(anchor[...], block, 1, 1)
    errors[:n, :] = errors_of(scores[:n], labels_o[...])
    errors[n:, :] = errors_of(scores[n:], labels_p[...])
    crossed = dot(turned[...], errors[...], 1, 0)
    part = dot(crossed.astype(narrow), block, 1, 0)

    @pl.when(j == 0)
    def _():
        term[...] = term_before[...] + part

    @pl.when(j > 0)
    def _():
        term[...] += part


def second(place, table_o, table_p, grad_o, grad_p, more_o, more_p, sums_o, sums_p, relation, items, targets, term, turn):
    n, d = table_o.shape
    m = items.shape[0]
    tile = pl.BlockSpec((TILE, d), lambda j, place: (j, 0))
    return call(
        second_body,
        "second",
        (m // TILE,),
        [whole(n, d)] * 6
        + [whole(1, n)] * 2
        + [
            whole(d, d),
            tile,
            pl.BlockSpec((None, n, TILE), lambda j, place: (turn, place[0], j)),
            pl.BlockSpec((None, n, TILE), lambda j, place: (turn, 1 - place[0], j)),
            whole(d, d),
        ],
        [
            whole(n, d),
            whole(1, n),
            whole(2 * n, d),
            pl.BlockSpec((2 * n, TILE), lambda j, place: (0, j)),
            whole(d, d),
        ],
        [
            shape(single, n, d),
            shape(single, 1, n),
            shape(narrow, 2 * n, d),
            shape(narrow, 2 * n, m),
            shape(single, d, d),
        ],
        [pltpu.VMEM((d, 2 * n), narrow)],
        4 * n * d * d + 8 * n * m * d + 2 * m * d * d,
        prefetch=1,
    )(place, table_o, table_p, grad_o, grad_p, more_o, more_p, sums_o, sums_p, relation, items, targets, targets, term)


def grads_body(errors, items, relation, grad_o, grad_p, total):
    j = pl.program_id(0)
    n = grad_o.shape[0]
    mapped = dot(items[...], relation[...], 1, 1).astype(narrow)
    part = dot(errors[...], mapped, 1, 0)

    @pl.when(j == 0)
    def _():
        total[...] = part

    @pl.when(j > 0)
    def _():
        total[...] += part

    @pl.when(j == pl.num_programs(0) - 1)
    def _():
        grad_o[...] = total[:n, :]
        grad_p[...] = total[n:, :].astype(narrow)


def second_grads(errors, items, relation):
    n = errors.shape[0] // 2
    m, d = items.shape
    return call(
        grads_body,
        "second_grads",
        (m // TILE,),
        [
            pl.BlockSpec((2 * n, TILE), lambda j: (0, j)),
            pl.BlockSpec((TILE, d), lambda j: (j, 0)),
            whole(d, d),
        ],
        [whole(n, d), whole(n, d)],
        [shape(single, n, d), shape(narrow, n, d)],
        [pltpu.VMEM((2 * n, d), single)],
        4 * n * m * d + 2 * m * d * d,
    )(errors, items, relation)


def users_body(table, grad, more, sums, table_next, sums_next):
    new, accum = adagrad_rows(table[...], as_column(sums[...]), grad[...] + wide(more[...]))
    table_next[...] = new
    sums_next[...] = as_line(accum)


def update_users(table, grad, more, sums):
    n, d = table.shape
    tile = pl.BlockSpec((TILE, d), lambda j: (j, 0))
    line = pl.BlockSpec((1, TILE), lambda j: (0, j))
    return call(
        users_body,
        "update_users",
        (n // TILE,),
        [tile, tile, tile, line],
        [tile, line],
        [shape(single, n, d), shape(single, 1, n)],
        [],
        4 * n * d,
    )(table, grad, more, sums)


def pick(parts, key):
    n = len(parts)
    level = 1
    while level < n:
        bit = (key // level) % 2 == 1
        parts = [jnp.where(bit, parts[k ^ level], parts[k]) for k in range(n)]
        level *= 2
    return jnp.concatenate(parts, axis=0)


def relation_total(p):
    blocks = lax.axis_size("blk")
    b, r = lax.axis_index("blk"), lax.axis_index("rel")
    core = b % 2
    with jax.named_scope("rel_core"):
        half = p.shape[0] // 2
        mine = lax.dynamic_slice_in_dim(p, core * half, half)
        other = lax.dynamic_slice_in_dim(p, (1 - core) * half, half)
        p = mine + exchange(other, 1, 0)
    with jax.named_scope("rel_xy"):
        key = r + 2 * ((b // 2) % 2)
        part = half // 4
        total = lax.dynamic_slice_in_dim(p, key * part, part)
        got = []
        for k in (3, 1, 2):
            piece = lax.dynamic_slice_in_dim(p, (key ^ k) * part, part).astype(narrow)
            got.append(wide(exchange(piece, 2 * (k // 2), k % 2)))
        total = total + (got[0] + (got[1] + got[2]))
    with jax.named_scope("rel_z"):
        flip = 4
        while blocks // flip > 8:
            sent = total.astype(narrow)
            total = wide(sent) + wide(exchange(sent, flip, 0))
            flip *= 2
        sent = total.astype(narrow)
        parts = [wide(sent)] + [wide(exchange(sent, flip * k, 0)) for k in range(1, blocks // flip)]
        while len(parts) > 1:
            parts = [parts[i] + parts[i + 1] for i in range(0, len(parts), 2)]
        sent = parts[0].astype(narrow)
    with jax.named_scope("rel_xy_back"):
        parts = [sent] + [exchange(sent, 2 * (k // 2), k % 2) for k in (1, 2, 3)]
        p = pick(parts, key)
    with jax.named_scope("rel_core_back"):
        return pick([p, exchange(p, 1, 0)], core)


def per_device(user_table, user_accum, item_table, item_accum, relation, relation_accum, targets):
    blocks = lax.axis_size("blk")
    rounds = targets.shape[0]
    assert rounds == 2 and lax.axis_size("rel") == 2
    place = lax.axis_index("rel").astype(jnp.int32).reshape(1)
    sums_o, item_sums = user_accum[None, :], item_accum[None, :]

    mine = user_table.astype(narrow)
    theirs = swap(mine)
    sums_p = swap(sums_o)
    items, mapped, anchor_o, errors_o, grad_o, grad_ob = first_own(
        place, mine, item_table, relation, targets, 0
    )
    more_p = swap(grad_ob)
    anchor_p, errors_p, grad_p, grad_pb = first_peer(place, theirs, items, mapped, relation, targets, 0)
    more_o = swap(grad_pb)
    items_next, item_sums = update_items(
        ((errors_o, 0), (errors_p, 0)), ((anchor_o, 0), (anchor_p, 0)), item_table, item_sums
    )
    items_next, item_sums = from_behind(items_next), from_behind(item_sums)
    term = first_term(mine, theirs, errors_o, errors_p, items)

    users, sums_o, anchor, errors, term = second(
        place, user_table, theirs, grad_o, grad_p, more_o, more_p, sums_o, sums_p,
        relation, items_next, targets, term, 1,
    )
    grad_o, grad_pb = second_grads(errors, items_next, relation)
    more_o = swap(grad_pb)
    items_last, item_sums = update_items(
        ((errors, 0), (errors, 1)), ((anchor, 0), (anchor, 1)), items_next, item_sums
    )
    items_last, item_sums = from_behind(items_last), from_behind(item_sums)
    users, sums_o = update_users(users, grad_o, more_o, sums_o)

    total = wide(relation_total(term))
    with jax.named_scope("rel_final"):
        mean_grad = total / (blocks * rounds)
        accum_next = relation_accum + jnp.mean(mean_grad * mean_grad, axis=1)
        relation_step = mean_grad * lax.rsqrt(accum_next + epsilon)[:, None]
    return (users, sums_o[0], wide(items_last), item_sums[0], relation_step, accum_next)


def solution(mesh):
    rows = P(("blk", "rel"), None)
    line = P(("blk", "rel"))
    return jax.shard_map(
        per_device,
        mesh=mesh,
        in_specs=(rows, line, rows, line, P(), P(), P(None, "blk", "rel")),
        out_specs=(rows, line, rows, line, P(), P()),
        check_vma=False,
    )
```

```python
import functools

import jax
import jax.numpy as jnp
from jax import lax
from jax.experimental import pallas as pl
from jax.experimental.pallas import tpu as pltpu
from jax.sharding import PartitionSpec as P


learn_rate = 0.1
epsilon = 1e-06
narrow = jnp.bfloat16
single = jnp.float32
TILE = 256


def exchange(x, flip, rel_flip):
    blocks, rels = lax.axis_size("blk"), lax.axis_size("rel")
    pairs = [
        (b * rels + r, (b ^ flip) * rels + (r ^ rel_flip)) for b in range(blocks) for r in range(rels)
    ]
    return lax.ppermute(x, ("blk", "rel"), pairs)


def swap(x):
    return exchange(x, 0, 1)


def from_behind(x):
    peers = lax.axis_size("blk")
    return lax.ppermute(x, "blk", [(i, (i + 1) % peers) for i in range(peers)])


def wide(x):
    return x.astype(single)


def dot(a, b, da, db):
    return lax.dot_general(a, b, (((da,), (db,)), ((), ())), preferred_element_type=single)


def as_column(line):
    return jnp.transpose(jnp.broadcast_to(line, (8, line.shape[1])))[:, :1]


def as_line(column):
    return jnp.transpose(jnp.broadcast_to(column, (column.shape[0], 128)))[:1, :]


def adagrad_rows(table, accum, grads):
    accum_next = accum + jnp.sum(grads * grads, axis=1, keepdims=True) * (1.0 / grads.shape[1])
    return table - grads * (learn_rate * lax.rsqrt(accum_next + epsilon)), accum_next


def whole(*shape):
    return pl.BlockSpec(shape, lambda *_: (0,) * len(shape))


def shape(dtype, *dims):
    return jax.ShapeDtypeStruct(dims, dtype)


def call(body, grid, in_specs, out_specs, out_shape, scratch, flops, prefetch=0, limit=63):
    return pl.pallas_call(
        body,
        grid_spec=pltpu.PrefetchScalarGridSpec(
            num_scalar_prefetch=prefetch,
            grid=grid,
            in_specs=in_specs,
            out_specs=out_specs,
            scratch_shapes=scratch,
        ),
        out_shape=out_shape,
        compiler_params=pltpu.CompilerParams(
            dimension_semantics=("arbitrary",) * len(grid), vmem_limit_bytes=limit << 20
        ),
        cost_estimate=pl.CostEstimate(flops=flops, bytes_accessed=4 << 20, transcendentals=0),
    )


def errors_of(scores, labels):
    return (jax.nn.sigmoid(scores) - wide(labels)).astype(narrow)


def anywhere():
    return pl.BlockSpec(memory_space=pl.ANY)


def manual(body, in_specs, out_specs, out_shape, scratch, copies, flops):
    return pl.pallas_call(
        body,
        in_specs=in_specs,
        out_specs=out_specs,
        out_shape=out_shape,
        scratch_shapes=[*scratch, pltpu.SemaphoreType.DMA((copies,))],
        compiler_params=pltpu.CompilerParams(vmem_limit_bytes=63 << 20),
        cost_estimate=pl.CostEstimate(flops=flops, bytes_accessed=4 << 20, transcendentals=0),
    )


class Copies:
    def __init__(self, sems):
        self.sems, self.used, self.out = sems, 0, []

    def start(self, source, target):
        copy = pltpu.make_async_copy(source, target, self.sems.at[self.used])
        self.used += 1
        copy.start()
        return copy

    def send(self, source, target):
        self.out.append(self.start(source, target))

    def finish(self):
        for copy in self.out:
            copy.wait()


def tiles(count):
    return [slice(k * TILE, (k + 1) * TILE) for k in range(count // TILE)]


def first_body(place, users, items, relation, labels, items_b, mapped, anchor, errors, grad, grad_b):
    j = pl.program_id(0)

    @pl.when(j == 0)
    def _():
        anchor[...] = dot(users[...], relation[...], 1, 0).astype(narrow)

    block = items[...].astype(narrow)
    items_b[...] = block
    mapped[...] = dot(block, relation[...], 1, 1).astype(narrow)
    found = errors_of(dot(anchor[...], block, 1, 1), labels[...])
    errors[...] = found
    part = dot(found, mapped[...], 1, 0)

    @pl.when(j == 0)
    def _():
        grad[...] = part

    @pl.when(j > 0)
    def _():
        grad[...] += part

    @pl.when(j == pl.num_programs(0) - 1)
    def _():
        grad_b[...] = grad[...].astype(narrow)


def first_own(place, users, items, relation, targets, turn):
    n, d = users.shape
    m = items.shape[0]
    tile = pl.BlockSpec((TILE, d), lambda j, place: (j, 0))
    labels = pl.BlockSpec((None, n, TILE), lambda j, place: (turn, place[0], j))
    return call(
        first_body,
        (m // TILE,),
        [whole(n, d), tile, whole(d, d), labels],
        [
            tile,
            tile,
            whole(n, d),
            pl.BlockSpec((n, TILE), lambda j, place: (0, j)),
            whole(n, d),
            whole(n, d),
        ],
        [
            shape(narrow, m, d),
            shape(narrow, m, d),
            shape(narrow, n, d),
            shape(narrow, n, m),
            shape(single, n, d),
            shape(narrow, n, d),
        ],
        [],
        2 * n * d * d + 2 * m * d * d + 4 * n * m * d,
        prefetch=1,
    )(place, users, items, relation, targets)


def peer_body(
    place, sums, users, relation, items_b, targets, mapped, errors_o, anchor_o, table,
    errors_p, grad_b, items_next, sums_next,
    v_users, v_relation, v_items, v_labels, v_mapped, v_errors_o, v_anchor_o, v_table,
    v_anchor, v_errors, v_grad, v_next, sems,
    turn,
):
    go = Copies(sems)
    n = users.shape[0]
    peer_rows = pl.ds(pl.multiple_of((1 - place[0]) * n, n), n)
    get_users = go.start(users, v_users)
    get_relation = go.start(relation, v_relation)
    get_items = go.start(items_b, v_items)
    get_labels = go.start(targets.at[turn, peer_rows], v_labels)
    get_mapped = go.start(mapped, v_mapped)
    get_errors = go.start(errors_o, v_errors_o)
    get_anchor = go.start(anchor_o, v_anchor_o)
    get_table = go.start(table, v_table)
    get_users.wait()
    get_relation.wait()
    v_anchor[...] = dot(v_users[...], v_relation[...], 1, 0).astype(narrow)
    get_items.wait()
    get_labels.wait()
    for at in tiles(v_items.shape[0]):
        scores = dot(v_anchor[...], v_items[at, :], 1, 1)
        v_errors[:, at] = errors_of(scores, v_labels[:, at])
    go.send(v_errors, errors_p)
    get_mapped.wait()
    v_grad[...] = dot(v_errors[...], v_mapped[...], 1, 0).astype(narrow)
    go.send(v_grad, grad_b)
    get_errors.wait()
    get_anchor.wait()
    get_table.wait()
    for at in tiles(v_items.shape[0]):
        grads = dot(v_errors_o[:, at], v_anchor_o[...], 0, 0) + dot(v_errors[:, at], v_anchor[...], 0, 0)
        new, accum = adagrad_rows(v_table[at, :], as_column(sums[:, at]), grads)
        v_next[at, :] = new.astype(narrow)
        sums_next[:, at] = as_line(accum)
        go.send(v_next.at[at, :], items_next.at[at, :])
    go.finish()


def first_peer(place, users, relation, items_b, targets, mapped, errors_o, anchor_o, table, sums, turn):
    n, d = users.shape
    m = table.shape[0]
    line = pl.BlockSpec(memory_space=pltpu.VMEM)
    return manual(
        functools.partial(peer_body, turn=turn),
        [pl.BlockSpec(memory_space=pltpu.SMEM), line] + [anywhere()] * 8,
        [anywhere()] * 3 + [line],
        [shape(narrow, n, m), shape(narrow, n, d), shape(narrow, m, d), shape(single, 1, m)],
        [
            pltpu.VMEM((n, d), narrow),
            pltpu.VMEM((d, d), narrow),
            pltpu.VMEM((m, d), narrow),
            pltpu.VMEM((n, m), narrow),
            pltpu.VMEM((m, d), narrow),
            pltpu.VMEM((n, m), narrow),
            pltpu.VMEM((n, d), narrow),
            pltpu.VMEM((m, d), single),
            pltpu.VMEM((n, d), narrow),
            pltpu.VMEM((n, m), narrow),
            pltpu.VMEM((n, d), narrow),
            pltpu.VMEM((m, d), narrow),
        ],
        10 + m // TILE,
        2 * n * d * d + 8 * n * m * d,
    )(place, sums, users, relation, items_b, targets, mapped, errors_o, anchor_o, table)


def ahead_body(table, grad, more, sums, relation, turned, anchor):
    new, _ = adagrad_rows(wide(table[...]), as_column(sums[...]), wide(grad[...]) + wide(more[...]))
    new = new.astype(narrow)
    turned[...] = jnp.transpose(new)
    anchor[...] = dot(new, relation[...], 1, 0).astype(narrow)


def ahead(table, grad, more, sums, relation):
    n, d = table.shape
    tile = pl.BlockSpec((TILE, d), lambda j: (j, 0))
    return call(
        ahead_body,
        (n // TILE,),
        [tile, tile, tile, pl.BlockSpec((1, TILE), lambda j: (0, j)), whole(d, d)],
        [pl.BlockSpec((d, TILE), lambda j: (0, j)), tile],
        [shape(narrow, d, n), shape(narrow, n, d)],
        [],
        2 * n * d * d,
    )(table, grad, more, sums, relation)


def term_body(users_o, users_p, errors_o, errors_p, items, term, turned_o, turned_p):
    j = pl.program_id(0)

    @pl.when(j == 0)
    def _():
        turned_o[...] = jnp.transpose(users_o[...])
        turned_p[...] = jnp.transpose(users_p[...])

    crossed = dot(turned_o[...], errors_o[...], 1, 0) + dot(turned_p[...], errors_p[...], 1, 0)
    part = dot(crossed.astype(narrow), items[...], 1, 0)

    @pl.when(j == 0)
    def _():
        term[...] = part

    @pl.when(j > 0)
    def _():
        term[...] += part


def first_term(users_o, users_p, errors_o, errors_p, items):
    n, d = users_o.shape
    m = items.shape[0]
    tile = pl.BlockSpec((TILE, d), lambda j: (j, 0))
    side = pl.BlockSpec((n, TILE), lambda j: (0, j))
    return call(
        term_body,
        (m // TILE,),
        [whole(n, d), whole(n, d), side, side, tile],
        whole(d, d),
        shape(single, d, d),
        [pltpu.VMEM((d, n), narrow), pltpu.VMEM((d, n), narrow)],
        4 * n * m * d + 2 * m * d * d,
    )(users_o, users_p, errors_o, errors_p, items)


def second_body(
    place, sums, item_sums, table, grad, more, relation, anchor_p, turned_p, items, targets, term,
    users_next, errors, term_keep, term_give, next_a, next_b, sums_next, item_sums_next,
    v_table, v_grad, v_more, v_relation, v_anchor, v_turned, v_items, v_labels, v_term,
    v_users, v_errors, v_crossed, v_next, sems,
    turn,
):
    go = Copies(sems)
    n, d = table.shape
    m = items.shape[0]
    get_more = go.start(more, v_more)
    get_table = go.start(table, v_table)
    get_grad = go.start(grad, v_grad)
    get_relation = go.start(relation, v_relation)
    get_anchor = go.start(anchor_p, v_anchor.at[n:, :])
    get_items, get_labels = [], []
    for at in tiles(m):
        get_items.append(go.start(items.at[at, :], v_items.at[at, :]))
        for half, first in ((0, place[0]), (1, 1 - place[0])):
            rows = pl.ds(pl.multiple_of(first * n, n), n)
            get_labels.append(
                go.start(targets.at[turn, rows, at], v_labels.at[half * n : half * n + n, at])
            )
    get_turned = go.start(turned_p, v_turned.at[:, n:])
    get_term = go.start(term, v_term)
    get_more.wait()
    get_table.wait()
    get_grad.wait()
    for at in tiles(n):
        new, accum = adagrad_rows(
            v_table[at, :], as_column(sums[:, at]), v_grad[at, :] + wide(v_more[at, :])
        )
        v_users[at, :] = new
        sums_next[:, at] = as_line(accum)
        v_turned[:, at] = jnp.transpose(new.astype(narrow))
    go.send(v_users, users_next)
    get_relation.wait()
    v_anchor[:n, :] = dot(v_users[...].astype(narrow), v_relation[...], 1, 0).astype(narrow)
    get_anchor.wait()
    for k, at in enumerate(tiles(m)):
        get_items[k].wait()
        get_labels[2 * k].wait()
        get_labels[2 * k + 1].wait()
        scores = dot(v_anchor[...], v_items[at, :], 1, 1)
        v_errors[:, at] = errors_of(scores, v_labels[:, at])
        go.send(v_errors.at[:, at], errors.at[:, at])
    get_turned.wait()
    get_term.wait()
    for at in tiles(d):
        v_crossed[at, :] = dot(v_turned[at, :], v_errors[...], 1, 0).astype(narrow)
        v_term[at, :] += dot(v_crossed[at, :], v_items[...], 1, 0)
    half = d // 2
    keep = pl.multiple_of(place[1] * half, half)
    give = pl.multiple_of((1 - place[1]) * half, half)
    go.send(v_term.at[pl.ds(give, half), :], term_give)
    go.send(v_term.at[pl.ds(keep, half), :], term_keep)
    for at in tiles(m):
        grads = dot(v_errors[:, at], v_anchor[...], 0, 0)
        new, accum = adagrad_rows(wide(v_items[at, :]), as_column(item_sums[:, at]), grads)
        v_next[at, :] = new.astype(narrow)
        item_sums_next[:, at] = as_line(accum)
        if at.start < m // 2:
            go.send(v_next.at[at, :], next_a.at[at, :])
        else:
            go.send(v_next.at[at, :], next_b.at[at.start - m // 2 : at.stop - m // 2, :])
    go.finish()


def second(place, table, grad, more, sums, relation, anchor_p, turned_p, items, item_sums, targets, term, turn):
    n, d = table.shape
    m = items.shape[0]
    line = pl.BlockSpec(memory_space=pltpu.VMEM)
    return manual(
        functools.partial(second_body, turn=turn),
        [pl.BlockSpec(memory_space=pltpu.SMEM), line, line] + [anywhere()] * 9,
        [anywhere()] * 6 + [line, line],
        [
            shape(single, n, d),
            shape(narrow, 2 * n, m),
            shape(single, d // 2, d),
            shape(single, d // 2, d),
            shape(narrow, m // 2, d),
            shape(narrow, m // 2, d),
            shape(single, 1, n),
            shape(single, 1, m),
        ],
        [
            pltpu.VMEM((n, d), single),
            pltpu.VMEM((n, d), single),
            pltpu.VMEM((n, d), narrow),
            pltpu.VMEM((d, d), narrow),
            pltpu.VMEM((2 * n, d), narrow),
            pltpu.VMEM((d, 2 * n), narrow),
            pltpu.VMEM((m, d), narrow),
            pltpu.VMEM((2 * n, m), narrow),
            pltpu.VMEM((d, d), single),
            pltpu.VMEM((n, d), single),
            pltpu.VMEM((2 * n, m), narrow),
            pltpu.VMEM((d, m), narrow),
            pltpu.VMEM((m, d), narrow),
        ],
        10 + 5 * (m // TILE),
        2 * n * d * d + 12 * n * m * d + 2 * m * d * d,
    )(place, sums, item_sums, table, grad, more, relation, anchor_p, turned_p, items, targets, term)


def grads_body(errors, items, relation, grad_o, grad_p,
               v_errors, v_items, v_relation, v_mapped, v_grad_o, v_grad_p, sems):
    go = Copies(sems)
    n = grad_o.shape[0]
    get_items = go.start(items, v_items)
    get_relation = go.start(relation, v_relation)
    rows = tiles(2 * n)
    order = rows[len(rows) // 2 :] + rows[: len(rows) // 2]
    get = [go.start(errors.at[at, :], v_errors.at[at, :]) for at in order]
    get_items.wait()
    get_relation.wait()
    v_mapped[...] = dot(v_items[...], v_relation[...], 1, 1).astype(narrow)
    for at, copy in zip(order, get):
        copy.wait()
        part = dot(v_errors[at, :], v_mapped[...], 1, 0)
        if at.start >= n:
            there = slice(at.start - n, at.stop - n)
            v_grad_p[there, :] = part.astype(narrow)
            go.send(v_grad_p.at[there, :], grad_p.at[there, :])
        else:
            v_grad_o[at, :] = part
            go.send(v_grad_o.at[at, :], grad_o.at[at, :])
    go.finish()


def second_grads(errors, items, relation):
    n = errors.shape[0] // 2
    m, d = items.shape
    return manual(
        grads_body,
        [anywhere()] * 3,
        [anywhere()] * 2,
        [shape(single, n, d), shape(narrow, n, d)],
        [
            pltpu.VMEM((2 * n, m), narrow),
            pltpu.VMEM((m, d), narrow),
            pltpu.VMEM((d, d), narrow),
            pltpu.VMEM((m, d), narrow),
            pltpu.VMEM((n, d), single),
            pltpu.VMEM((n, d), narrow),
        ],
        2 + 4 * (n // TILE),
        4 * n * m * d + 2 * m * d * d,
    )(errors, items, relation)


def users_body(table, grad, more, sums, table_next, sums_next):
    new, accum = adagrad_rows(table[...], as_column(sums[...]), grad[...] + wide(more[...]))
    table_next[...] = new
    sums_next[...] = as_line(accum)


def update_users(table, grad, more, sums):
    n, d = table.shape
    tile = pl.BlockSpec((TILE, d), lambda j: (j, 0))
    line = pl.BlockSpec((1, TILE), lambda j: (0, j))
    return call(
        users_body,
        (n // TILE,),
        [tile, tile, tile, line],
        [tile, line],
        [shape(single, n, d), shape(single, 1, n)],
        [],
        4 * n * d,
    )(table, grad, more, sums)


def pick(parts, key):
    n = len(parts)
    level = 1
    while level < n:
        bit = (key // level) % 2 == 1
        parts = [jnp.where(bit, parts[k ^ level], parts[k]) for k in range(n)]
        level *= 2
    return jnp.concatenate(parts, axis=0)


def relation_total(keep, give):
    blocks = lax.axis_size("blk")
    b, r = lax.axis_index("blk"), lax.axis_index("rel")
    core = b % 2
    half = keep.shape[0]
    p = keep + exchange(give, 1, 0)
    key = r + 2 * ((b // 2) % 2)
    part = half // 4
    total = lax.dynamic_slice_in_dim(p, key * part, part)
    got = []
    for k in (3, 1, 2):
        piece = lax.dynamic_slice_in_dim(p, (key ^ k) * part, part).astype(narrow)
        got.append(wide(exchange(piece, 2 * (k // 2), k % 2)))
    total = total + (got[0] + (got[1] + got[2]))
    flip = 4
    while blocks // flip > 8:
        sent = total.astype(narrow)
        total = wide(sent) + wide(exchange(sent, flip, 0))
        flip *= 2
    sent = total.astype(narrow)
    parts = [wide(sent)]
    for k in range(1, blocks // flip):
        parts.append(wide(exchange(sent, flip * k, 0)))
    while len(parts) > 1:
        parts = [parts[i] + parts[i + 1] for i in range(0, len(parts), 2)]
    sent = parts[0].astype(narrow)
    parts = [sent] + [exchange(sent, 2 * (k // 2), k % 2) for k in (1, 2, 3)]
    p = pick(parts, key)
    return pick([p, exchange(p, 1, 0)], core)


def step(user_table, user_accum, item_table, item_accum, relation, relation_accum, targets):
    blocks = lax.axis_size("blk")
    rounds = targets.shape[0]
    assert rounds == 2 and lax.axis_size("rel") == 2
    place = jnp.stack([lax.axis_index("rel"), lax.axis_index("blk") % 2]).astype(jnp.int32)
    sums_o, item_sums = user_accum[None, :], item_accum[None, :]

    mine = user_table.astype(narrow)
    theirs = swap(mine)
    items, mapped, anchor_o, errors_o, grad_o, grad_ob = first_own(
        place[:1], mine, item_table, relation, targets, 0
    )
    more_p = swap(grad_ob)
    sums_p = swap(sums_o)
    errors_p, grad_pb, items_next, item_sums = first_peer(
        place, theirs, relation, items, targets, mapped, errors_o, anchor_o, item_table, item_sums, 0
    )
    more_o = swap(grad_pb)
    items_next = from_behind(items_next)
    item_sums = from_behind(item_sums)
    term = first_term(mine, theirs, errors_o, errors_p, items)
    turned_p, anchor_p = ahead(theirs, grad_pb, more_p, sums_p, relation)

    users, errors, keep, give, *chunks, sums_o, item_sums = second(
        place, user_table, grad_o, more_o, sums_o, relation, anchor_p, turned_p,
        items_next, item_sums, targets, term, 1,
    )
    grad_o, grad_pb = second_grads(errors, items_next, relation)
    more_o = swap(grad_pb)
    chunks = [from_behind(chunk) for chunk in chunks]
    item_sums = from_behind(item_sums)
    users, sums_o = update_users(users, grad_o, more_o, sums_o)

    total = wide(relation_total(keep, give))
    mean_grad = total / (blocks * rounds)
    accum_next = relation_accum + jnp.mean(mean_grad * mean_grad, axis=1)
    relation_step = mean_grad * lax.rsqrt(accum_next + epsilon)[:, None]
    items_last = jnp.concatenate([wide(chunk) for chunk in chunks], axis=0)
    return (users, sums_o[0], items_last, item_sums[0], relation_step, accum_next)


def solution(mesh):
    rows = P(("blk", "rel"), None)
    line = P(("blk", "rel"))
    return jax.shard_map(
        step,
        mesh=mesh,
        in_specs=(rows, line, rows, line, P(), P(), P(None, "blk", "rel")),
        out_specs=(rows, line, rows, line, P(), P()),
        check_vma=False,
    )
```

```python
import functools

import jax
import jax.numpy as jnp
from jax import lax
from jax.experimental import pallas as pl
from jax.experimental.pallas import tpu as pltpu
from jax.sharding import PartitionSpec as P


learn_rate = 0.1
epsilon = 1e-06
narrow = jnp.bfloat16
single = jnp.float32
TILE = 256


def exchange(x, flip, rel_flip):
    blocks, rels = lax.axis_size("blk"), lax.axis_size("rel")
    pairs = [
        (b * rels + r, (b ^ flip) * rels + (r ^ rel_flip)) for b in range(blocks) for r in range(rels)
    ]
    return lax.ppermute(x, ("blk", "rel"), pairs)


def swap(x):
    return exchange(x, 0, 1)


def from_behind(x):
    peers = lax.axis_size("blk")
    return lax.ppermute(x, "blk", [(i, (i + 1) % peers) for i in range(peers)])


def wide(x):
    return x.astype(single)


def dot(a, b, da, db):
    return lax.dot_general(a, b, (((da,), (db,)), ((), ())), preferred_element_type=single)


def as_column(line):
    return jnp.transpose(jnp.broadcast_to(line, (8, line.shape[1])))[:, :1]


def as_line(column):
    return jnp.transpose(jnp.broadcast_to(column, (column.shape[0], 128)))[:1, :]


def adagrad_rows(table, accum, grads):
    accum_next = accum + jnp.sum(grads * grads, axis=1, keepdims=True) * (1.0 / grads.shape[1])
    return table - grads * (learn_rate * lax.rsqrt(accum_next + epsilon)), accum_next


def columns_into(scratch, line):
    scratch[...] = jnp.transpose(jnp.broadcast_to(line, (8, line.shape[1])))


def whole(*shape):
    return pl.BlockSpec(shape, lambda *_: (0,) * len(shape))


def shape(dtype, *dims):
    return jax.ShapeDtypeStruct(dims, dtype)


def call(body, grid, in_specs, out_specs, out_shape, scratch, flops, prefetch=0, limit=63):
    return pl.pallas_call(
        body,
        grid_spec=pltpu.PrefetchScalarGridSpec(
            num_scalar_prefetch=prefetch,
            grid=grid,
            in_specs=in_specs,
            out_specs=out_specs,
            scratch_shapes=scratch,
        ),
        out_shape=out_shape,
        compiler_params=pltpu.CompilerParams(
            dimension_semantics=("arbitrary",) * len(grid), vmem_limit_bytes=limit << 20
        ),
        cost_estimate=pl.CostEstimate(flops=flops, bytes_accessed=4 << 20, transcendentals=0),
    )


def errors_of(scores, labels):
    return (jax.nn.sigmoid(scores) - wide(labels)).astype(narrow)


def anywhere():
    return pl.BlockSpec(memory_space=pl.ANY)


def manual(body, in_specs, out_specs, out_shape, scratch, copies, flops):
    return pl.pallas_call(
        body,
        in_specs=in_specs,
        out_specs=out_specs,
        out_shape=out_shape,
        scratch_shapes=[*scratch, pltpu.SemaphoreType.DMA((copies,))],
        compiler_params=pltpu.CompilerParams(vmem_limit_bytes=63 << 20),
        cost_estimate=pl.CostEstimate(flops=flops, bytes_accessed=4 << 20, transcendentals=0),
    )


class Copies:
    def __init__(self, sems):
        self.sems, self.used, self.out = sems, 0, []

    def start(self, source, target):
        copy = pltpu.make_async_copy(source, target, self.sems.at[self.used])
        self.used += 1
        copy.start()
        return copy

    def send(self, source, target):
        self.out.append(self.start(source, target))

    def finish(self):
        for copy in self.out:
            copy.wait()


def tiles(count):
    return [slice(k * TILE, (k + 1) * TILE) for k in range(count // TILE)]


def first_body(place, users, items, relation, labels, items_b, mapped, anchor, errors, grad_b, grad):
    j = pl.program_id(0)

    @pl.when(j == 0)
    def _():
        anchor[...] = dot(users[...], relation[...], 1, 0).astype(narrow)

    block = items[...].astype(narrow)
    items_b[...] = block
    mapped[...] = dot(block, relation[...], 1, 1).astype(narrow)
    found = errors_of(dot(anchor[...], block, 1, 1), labels[...])
    errors[...] = found
    part = dot(found, mapped[...], 1, 0)

    @pl.when(j == 0)
    def _():
        grad[...] = part

    @pl.when(j > 0)
    def _():
        grad[...] += part

    @pl.when(j == pl.num_programs(0) - 1)
    def _():
        grad_b[...] = grad[...].astype(narrow)


def first_own(place, users, items, relation, targets, turn):
    n, d = users.shape
    m = items.shape[0]
    tile = pl.BlockSpec((TILE, d), lambda j, place: (j, 0))
    labels = pl.BlockSpec((None, n, TILE), lambda j, place: (turn, place[0], j))
    return call(
        first_body,
        (m // TILE,),
        [whole(n, d), tile, whole(d, d), labels],
        [
            tile,
            tile,
            whole(n, d),
            pl.BlockSpec((n, TILE), lambda j, place: (0, j)),
            whole(n, d),
        ],
        [
            shape(narrow, m, d),
            shape(narrow, m, d),
            shape(narrow, n, d),
            shape(narrow, n, m),
            shape(narrow, n, d),
        ],
        [pltpu.VMEM((n, d), single)],
        2 * n * d * d + 2 * m * d * d + 4 * n * m * d,
        prefetch=1,
    )(place, users, items, relation, targets)


def peer_body(
    place, sums, users, relation, items_b, targets, mapped, errors_o, anchor_o, table,
    users_b, errors_p, grad_b, items_next, sums_next,
    v_relation, v_items, v_labels, v_mapped, v_errors_o, v_anchor_o, v_table,
    v_anchor, v_errors, v_grad, v_next, v_sums, v_lines, sems,
    turn,
):
    go = Copies(sems)
    n = users.shape[0]
    peer_rows = pl.ds(pl.multiple_of((1 - place[0]) * n, n), n)
    get_relation = go.start(relation, v_relation)
    go.send(users, users_b)
    get_items = go.start(items_b, v_items)
    get_labels = go.start(targets.at[turn, peer_rows], v_labels)
    get_mapped = go.start(mapped, v_mapped)
    get_errors = go.start(errors_o, v_errors_o)
    get_anchor = go.start(anchor_o, v_anchor_o)
    get_table = go.start(table, v_table)
    columns_into(v_sums, sums[...])
    get_relation.wait()
    v_anchor[...] = dot(users[...], v_relation[...], 1, 0).astype(narrow)
    get_items.wait()
    get_labels.wait()
    for at in tiles(v_items.shape[0]):
        scores = dot(v_anchor[...], v_items[at, :], 1, 1)
        v_errors[:, at] = errors_of(scores, v_labels[:, at])
    go.send(v_errors, errors_p)
    get_mapped.wait()
    v_grad[...] = dot(v_errors[...], v_mapped[...], 1, 0).astype(narrow)
    go.send(v_grad, grad_b)
    get_errors.wait()
    get_anchor.wait()
    get_table.wait()
    for at in tiles(v_items.shape[0]):
        grads = dot(v_errors_o[:, at], v_anchor_o[...], 0, 0) + dot(v_errors[:, at], v_anchor[...], 0, 0)
        new, accum = adagrad_rows(v_table[at, :], v_sums[at, :1], grads)
        v_next[at, :] = new.astype(narrow)
        v_lines[at, :] = jnp.broadcast_to(accum, (TILE, 128))
        go.send(v_next.at[at, :], items_next.at[at, :])
    for at in tiles(v_items.shape[0]):
        sums_next[:, at] = jnp.transpose(v_lines[at, :])[:1, :]
    go.finish()


def first_peer(place, users, relation, items_b, targets, mapped, errors_o, anchor_o, table, sums, turn):
    n, d = users.shape
    m = table.shape[0]
    line = pl.BlockSpec(memory_space=pltpu.VMEM)
    return manual(
        functools.partial(peer_body, turn=turn),
        [pl.BlockSpec(memory_space=pltpu.SMEM), line, line] + [anywhere()] * 7,
        [anywhere()] * 4 + [line],
        [
            shape(narrow, n, d),
            shape(narrow, n, m),
            shape(narrow, n, d),
            shape(narrow, m, d),
            shape(single, 1, m),
        ],
        [
            pltpu.VMEM((d, d), narrow),
            pltpu.VMEM((m, d), narrow),
            pltpu.VMEM((n, m), narrow),
            pltpu.VMEM((m, d), narrow),
            pltpu.VMEM((n, m), narrow),
            pltpu.VMEM((n, d), narrow),
            pltpu.VMEM((m, d), single),
            pltpu.VMEM((n, d), narrow),
            pltpu.VMEM((n, m), narrow),
            pltpu.VMEM((n, d), narrow),
            pltpu.VMEM((m, d), narrow),
            pltpu.VMEM((m, 8), single),
            pltpu.VMEM((m, 128), single),
        ],
        10 + m // TILE,
        2 * n * d * d + 8 * n * m * d,
    )(place, sums, users, relation, items_b, targets, mapped, errors_o, anchor_o, table)


def ahead_body(table, grad, more, sums, relation, turned, anchor):
    new, _ = adagrad_rows(wide(table[...]), as_column(sums[...]), wide(grad[...]) + wide(more[...]))
    new = new.astype(narrow)
    turned[...] = jnp.transpose(new)
    anchor[...] = dot(new, relation[...], 1, 0).astype(narrow)


def ahead(table, grad, more, sums, relation):
    n, d = table.shape
    tile = pl.BlockSpec((TILE, d), lambda j: (j, 0))
    return call(
        ahead_body,
        (n // TILE,),
        [tile, tile, tile, pl.BlockSpec((1, TILE), lambda j: (0, j)), whole(d, d)],
        [pl.BlockSpec((d, TILE), lambda j: (0, j)), tile],
        [shape(narrow, d, n), shape(narrow, n, d)],
        [],
        2 * n * d * d,
    )(table, grad, more, sums, relation)


def term_body(users_o, users_p, errors_o, errors_p, items, term, turned_o, turned_p):
    j = pl.program_id(0)

    @pl.when(j == 0)
    def _():
        turned_o[...] = jnp.transpose(users_o[...])
        turned_p[...] = jnp.transpose(users_p[...])

    crossed = dot(turned_o[...], errors_o[...], 1, 0) + dot(turned_p[...], errors_p[...], 1, 0)
    part = dot(crossed.astype(narrow), items[...], 1, 0)

    @pl.when(j == 0)
    def _():
        term[...] = part

    @pl.when(j > 0)
    def _():
        term[...] += part


def first_term(users_o, users_p, errors_o, errors_p, items):
    n, d = users_o.shape
    m = items.shape[0]
    tile = pl.BlockSpec((TILE, d), lambda j: (j, 0))
    side = pl.BlockSpec((n, TILE), lambda j: (0, j))
    return call(
        term_body,
        (m // TILE,),
        [whole(n, d), whole(n, d), side, side, tile],
        whole(d, d),
        shape(single, d, d),
        [pltpu.VMEM((d, n), narrow), pltpu.VMEM((d, n), narrow)],
        4 * n * m * d + 2 * m * d * d,
    )(users_o, users_p, errors_o, errors_p, items)


def second_body(
    place, sums, item_sums, table, grad, more, relation, anchor_p, turned_p, items, targets, term,
    users_next, errors, term_keep, term_give, next_a, next_b, sums_next, item_sums_next,
    v_table, v_grad, v_more, v_relation, v_anchor, v_turned, v_items, v_labels, v_term,
    v_users, v_errors, v_crossed, v_next, v_sums, v_lines, sems,
    turn,
):
    go = Copies(sems)
    n, d = table.shape
    m = items.shape[0]
    get_table = []
    for at in tiles(n):
        for source, target in ((more, v_more), (grad, v_grad), (table, v_table)):
            get_table.append(go.start(source.at[at, :], target.at[at, :]))
    get_relation = go.start(relation, v_relation)
    get_anchor = go.start(anchor_p, v_anchor.at[n:, :])
    get_items, get_labels = [], []
    for at in tiles(m):
        get_items.append(go.start(items.at[at, :], v_items.at[at, :]))
        for half, first in ((0, place[0]), (1, 1 - place[0])):
            rows = pl.ds(pl.multiple_of(first * n, n), n)
            get_labels.append(
                go.start(targets.at[turn, rows, at], v_labels.at[half * n : half * n + n, at])
            )
    get_turned = go.start(turned_p, v_turned.at[:, n:])
    get_term = go.start(term, v_term)
    columns_into(v_sums.at[:n, :], sums[...])
    columns_into(v_sums.at[n:, :], item_sums[...])
    for k, at in enumerate(tiles(n)):
        for copy in get_table[3 * k : 3 * k + 3]:
            copy.wait()
        new, accum = adagrad_rows(
            v_table[at, :], v_sums[at, :1], wide(v_grad[at, :]) + wide(v_more[at, :])
        )
        v_users[at, :] = new
        v_lines[at, :] = jnp.broadcast_to(accum, (TILE, 128))
        v_turned[:, at] = jnp.transpose(new.astype(narrow))
    go.send(v_users, users_next)
    get_relation.wait()
    v_anchor[:n, :] = dot(v_users[...].astype(narrow), v_relation[...], 1, 0).astype(narrow)
    get_anchor.wait()
    for k, at in enumerate(tiles(m)):
        get_items[k].wait()
        get_labels[2 * k].wait()
        get_labels[2 * k + 1].wait()
        scores = dot(v_anchor[...], v_items[at, :], 1, 1)
        v_errors[:, at] = errors_of(scores, v_labels[:, at])
        go.send(v_errors.at[:, at], errors.at[:, at])
    get_turned.wait()
    get_term.wait()
    for at in tiles(d):
        v_crossed[at, :] = dot(v_turned[at, :], v_errors[...], 1, 0).astype(narrow)
        v_term[at, :] += dot(v_crossed[at, :], v_items[...], 1, 0)
    half = d // 2
    keep = pl.multiple_of(place[1] * half, half)
    give = pl.multiple_of((1 - place[1]) * half, half)
    go.send(v_term.at[pl.ds(give, half), :], term_give)
    go.send(v_term.at[pl.ds(keep, half), :], term_keep)
    for at in tiles(m):
        grads = dot(v_errors[:, at], v_anchor[...], 0, 0)
        below = slice(n + at.start, n + at.stop)
        new, accum = adagrad_rows(wide(v_items[at, :]), v_sums[below, :1], grads)
        v_next[at, :] = new.astype(narrow)
        v_lines[below, :] = jnp.broadcast_to(accum, (TILE, 128))
        if at.start < m // 2:
            go.send(v_next.at[at, :], next_a.at[at, :])
        else:
            go.send(v_next.at[at, :], next_b.at[at.start - m // 2 : at.stop - m // 2, :])
    for at in tiles(n + m):
        line = jnp.transpose(v_lines[at, :])[:1, :]
        if at.start < n:
            sums_next[:, at] = line
        else:
            item_sums_next[:, at.start - n : at.stop - n] = line
    go.finish()


def second(place, table, grad, more, sums, relation, anchor_p, turned_p, items, item_sums, targets, term, turn):
    n, d = table.shape
    m = items.shape[0]
    line = pl.BlockSpec(memory_space=pltpu.VMEM)
    return manual(
        functools.partial(second_body, turn=turn),
        [pl.BlockSpec(memory_space=pltpu.SMEM), line, line] + [anywhere()] * 9,
        [anywhere()] * 6 + [line, line],
        [
            shape(single, n, d),
            shape(narrow, 2 * n, m),
            shape(single, d // 2, d),
            shape(single, d // 2, d),
            shape(narrow, m // 2, d),
            shape(narrow, m // 2, d),
            shape(single, 1, n),
            shape(single, 1, m),
        ],
        [
            pltpu.VMEM((n, d), single),
            pltpu.VMEM((n, d), narrow),
            pltpu.VMEM((n, d), narrow),
            pltpu.VMEM((d, d), narrow),
            pltpu.VMEM((2 * n, d), narrow),
            pltpu.VMEM((d, 2 * n), narrow),
            pltpu.VMEM((m, d), narrow),
            pltpu.VMEM((2 * n, m), narrow),
            pltpu.VMEM((d, d), single),
            pltpu.VMEM((n, d), single),
            pltpu.VMEM((2 * n, m), narrow),
            pltpu.VMEM((d, m), narrow),
            pltpu.VMEM((m, d), narrow),
            pltpu.VMEM((n + m, 8), single),
            pltpu.VMEM((n + m, 128), single),
        ],
        8 + 3 * (n // TILE) + 5 * (m // TILE),
        2 * n * d * d + 12 * n * m * d + 2 * m * d * d,
    )(place, sums, item_sums, table, grad, more, relation, anchor_p, turned_p, items, targets, term)


def grads_body(errors, items, relation, grad_o, grad_p,
               v_errors, v_items, v_relation, v_mapped, v_grad_o, v_grad_p, sems):
    go = Copies(sems)
    n = grad_o.shape[0]
    get_items = go.start(items, v_items)
    get_relation = go.start(relation, v_relation)
    rows = tiles(2 * n)
    order = rows[len(rows) // 2 :] + rows[: len(rows) // 2]
    get = [go.start(errors.at[at, :], v_errors.at[at, :]) for at in order]
    get_items.wait()
    get_relation.wait()
    v_mapped[...] = dot(v_items[...], v_relation[...], 1, 1).astype(narrow)
    for at, copy in zip(order, get):
        copy.wait()
        part = dot(v_errors[at, :], v_mapped[...], 1, 0)
        if at.start >= n:
            there = slice(at.start - n, at.stop - n)
            v_grad_p[there, :] = part.astype(narrow)
            go.send(v_grad_p.at[there, :], grad_p.at[there, :])
        else:
            v_grad_o[at, :] = part
            go.send(v_grad_o.at[at, :], grad_o.at[at, :])
    go.finish()


def second_grads(errors, items, relation):
    n = errors.shape[0] // 2
    m, d = items.shape
    return manual(
        grads_body,
        [anywhere()] * 3,
        [anywhere()] * 2,
        [shape(single, n, d), shape(narrow, n, d)],
        [
            pltpu.VMEM((2 * n, m), narrow),
            pltpu.VMEM((m, d), narrow),
            pltpu.VMEM((d, d), narrow),
            pltpu.VMEM((m, d), narrow),
            pltpu.VMEM((n, d), single),
            pltpu.VMEM((n, d), narrow),
        ],
        2 + 4 * (n // TILE),
        4 * n * m * d + 2 * m * d * d,
    )(errors, items, relation)


def users_body(table, grad, more, sums, table_next, sums_next):
    new, accum = adagrad_rows(table[...], as_column(sums[...]), grad[...] + wide(more[...]))
    table_next[...] = new
    sums_next[...] = as_line(accum)


def update_users(table, grad, more, sums):
    n, d = table.shape
    tile = pl.BlockSpec((TILE, d), lambda j: (j, 0))
    line = pl.BlockSpec((1, TILE), lambda j: (0, j))
    return call(
        users_body,
        (n // TILE,),
        [tile, tile, tile, line],
        [tile, line],
        [shape(single, n, d), shape(single, 1, n)],
        [],
        4 * n * d,
        limit=16,
    )(table, grad, more, sums)


def final_body(place, mine, other, sums, step, sums_next, *, count):
    half = mine.shape[0]
    for part, side in ((mine, place[1]), (other, 1 - place[1])):
        rows = pl.ds(pl.multiple_of(side * half, half), half)
        grads = wide(part[...]) / count
        _, accum = adagrad_rows(grads, as_column(sums[:, rows]), grads)
        step[rows, :] = grads * lax.rsqrt(accum + epsilon)
        sums_next[:, rows] = as_line(accum)


def final(place, mine, other, sums, count):
    d = mine.shape[1]
    whole_array = pl.BlockSpec(memory_space=pltpu.VMEM)
    return pl.pallas_call(
        functools.partial(final_body, count=count),
        name="final",
        in_specs=[pl.BlockSpec(memory_space=pltpu.SMEM)] + [whole_array] * 3,
        out_specs=[whole_array] * 2,
        out_shape=[shape(single, d, d), shape(single, 1, d)],
        compiler_params=pltpu.CompilerParams(vmem_limit_bytes=16 << 20),
    )(place, mine, other, sums)


def pick(parts, key):
    n = len(parts)
    level = 1
    while level < n:
        bit = (key // level) % 2 == 1
        parts = [jnp.where(bit, parts[k ^ level], parts[k]) for k in range(n)]
        level *= 2
    return jnp.concatenate(parts, axis=0)


def relation_total(keep, give):
    blocks = lax.axis_size("blk")
    b, r = lax.axis_index("blk"), lax.axis_index("rel")
    half = keep.shape[0]
    p = keep + exchange(give, 1, 0)
    key = r + 2 * ((b // 2) % 2)
    part = half // 4
    total = lax.dynamic_slice_in_dim(p, key * part, part)
    got = []
    for k in (3, 1, 2):
        piece = lax.dynamic_slice_in_dim(p, (key ^ k) * part, part).astype(narrow)
        got.append(wide(exchange(piece, 2 * (k // 2), k % 2)))
    total = total + (got[0] + (got[1] + got[2]))
    flip = 4
    while blocks // flip > 8:
        sent = total.astype(narrow)
        total = wide(sent) + wide(exchange(sent, flip, 0))
        flip *= 2
    sent = total.astype(narrow)
    parts = [wide(sent)]
    for k in range(1, blocks // flip):
        parts.append(wide(exchange(sent, flip * k, 0)))
    while len(parts) > 1:
        parts = [parts[i] + parts[i + 1] for i in range(0, len(parts), 2)]
    sent = parts[0].astype(narrow)
    parts = [sent] + [exchange(sent, 2 * (k // 2), k % 2) for k in (1, 2, 3)]
    p = pick(parts, key)
    return p, exchange(p, 1, 0)


def step(user_table, user_accum, item_table, item_accum, relation, relation_accum, targets):
    blocks = lax.axis_size("blk")
    rounds = targets.shape[0]
    assert rounds == 2 and lax.axis_size("rel") == 2
    place = jnp.stack([lax.axis_index("rel"), lax.axis_index("blk") % 2]).astype(jnp.int32)
    sums_o, item_sums = user_accum[None, :], item_accum[None, :]

    mine = user_table.astype(narrow)
    theirs = swap(mine)
    items, mapped, anchor_o, errors_o, grad_ob = first_own(
        place[:1], mine, item_table, relation, targets, 0
    )
    more_p = swap(grad_ob)
    sums_p = swap(sums_o)
    users_p, errors_p, grad_pb, items_next, item_sums = first_peer(
        place, theirs, relation, items, targets, mapped, errors_o, anchor_o, item_table, item_sums, 0
    )
    more_o = swap(grad_pb)
    items_next = from_behind(items_next)
    item_sums = from_behind(item_sums)
    term = first_term(mine, users_p, errors_o, errors_p, items)
    turned_p, anchor_p = ahead(users_p, grad_pb, more_p, sums_p, relation)

    users, errors, keep, give, *chunks, sums_o, item_sums = second(
        place, user_table, grad_ob, more_o, sums_o, relation, anchor_p, turned_p,
        items_next, item_sums, targets, term, 1,
    )
    grad_o, grad_pb = second_grads(errors, items_next, relation)
    more_o = swap(grad_pb)
    chunks = [from_behind(chunk) for chunk in chunks]
    item_sums = from_behind(item_sums)
    users, sums_o = update_users(users, grad_o, more_o, sums_o)

    relation_step, accum_next = final(
        place, *relation_total(keep, give), relation_accum[None, :], blocks * rounds
    )
    items_last = jnp.concatenate([wide(chunk) for chunk in chunks], axis=0)
    item_sums = jnp.maximum(item_sums[0], 0.0)
    return (users, sums_o[0], items_last, item_sums, relation_step, accum_next[0])


def solution(mesh):
    rows = P(("blk", "rel"), None)
    line = P(("blk", "rel"))
    return jax.shard_map(
        step,
        mesh=mesh,
        in_specs=(rows, line, rows, line, P(), P(), P(None, "blk", "rel")),
        out_specs=(rows, line, rows, line, P(), P()),
        check_vma=False,
    )
```

```python
import functools

import jax
import jax.numpy as jnp
from jax import lax
from jax.experimental import pallas as pl
from jax.experimental.pallas import tpu as pltpu
from jax.sharding import PartitionSpec as P


learn_rate = 0.1
epsilon = 1e-06
narrow = jnp.bfloat16
single = jnp.float32
TILE = 256


def exchange(x, flip, rel_flip):
    blocks, rels = lax.axis_size("blk"), lax.axis_size("rel")
    pairs = [
        (b * rels + r, (b ^ flip) * rels + (r ^ rel_flip)) for b in range(blocks) for r in range(rels)
    ]
    return lax.ppermute(x, ("blk", "rel"), pairs)


def swap(x):
    return exchange(x, 0, 1)


def from_behind(x):
    peers = lax.axis_size("blk")
    return lax.ppermute(x, "blk", [(i, (i + 1) % peers) for i in range(peers)])


def wide(x):
    return x.astype(single)


def dot(a, b, da, db):
    return lax.dot_general(a, b, (((da,), (db,)), ((), ())), preferred_element_type=single)


def as_column(line):
    return jnp.transpose(jnp.broadcast_to(line, (8, line.shape[1])))[:, :1]


def as_line(column):
    return jnp.transpose(jnp.broadcast_to(column, (column.shape[0], 128)))[:1, :]


def adagrad_rows(table, accum, grads):
    accum_next = accum + jnp.sum(grads * grads, axis=1, keepdims=True) * (1.0 / grads.shape[1])
    return table - grads * (learn_rate * lax.rsqrt(accum_next + epsilon)), accum_next


def columns_into(scratch, line):
    scratch[...] = jnp.transpose(jnp.broadcast_to(line, (8, line.shape[1])))


def whole(*shape):
    return pl.BlockSpec(shape, lambda *_: (0,) * len(shape))


def shape(dtype, *dims):
    return jax.ShapeDtypeStruct(dims, dtype)


def call(body, grid, in_specs, out_specs, out_shape, scratch, flops, prefetch=0, limit=63):
    return pl.pallas_call(
        body,
        grid_spec=pltpu.PrefetchScalarGridSpec(
            num_scalar_prefetch=prefetch,
            grid=grid,
            in_specs=in_specs,
            out_specs=out_specs,
            scratch_shapes=scratch,
        ),
        out_shape=out_shape,
        compiler_params=pltpu.CompilerParams(
            dimension_semantics=("arbitrary",) * len(grid), vmem_limit_bytes=limit << 20
        ),
        cost_estimate=pl.CostEstimate(flops=flops, bytes_accessed=4 << 20, transcendentals=0),
    )


def errors_of(scores, labels):
    return (jax.nn.sigmoid(scores) - wide(labels)).astype(narrow)


def anywhere():
    return pl.BlockSpec(memory_space=pl.ANY)


def manual(body, in_specs, out_specs, out_shape, scratch, copies, flops):
    return pl.pallas_call(
        body,
        in_specs=in_specs,
        out_specs=out_specs,
        out_shape=out_shape,
        scratch_shapes=[*scratch, pltpu.SemaphoreType.DMA((copies,))],
        compiler_params=pltpu.CompilerParams(vmem_limit_bytes=63 << 20),
        cost_estimate=pl.CostEstimate(flops=flops, bytes_accessed=4 << 20, transcendentals=0),
    )


class Copies:
    def __init__(self, sems):
        self.sems, self.used, self.out = sems, 0, []

    def start(self, source, target):
        copy = pltpu.make_async_copy(source, target, self.sems.at[self.used])
        self.used += 1
        copy.start()
        return copy

    def send(self, source, target):
        self.out.append(self.start(source, target))

    def finish(self):
        for copy in self.out:
            copy.wait()


def tiles(count):
    return [slice(k * TILE, (k + 1) * TILE) for k in range(count // TILE)]


def first_body(place, users, items, relation, labels, items_b, mapped, anchor, errors, grad_b, grad):
    j = pl.program_id(0)

    @pl.when(j == 0)
    def _():
        anchor[...] = dot(users[...], relation[...], 1, 0).astype(narrow)

    block = items[...].astype(narrow)
    items_b[...] = block
    mapped[...] = dot(block, relation[...], 1, 1).astype(narrow)
    found = errors_of(dot(anchor[...], block, 1, 1), labels[...])
    errors[...] = found
    part = dot(found, mapped[...], 1, 0)

    @pl.when(j == 0)
    def _():
        grad[...] = part

    @pl.when(j > 0)
    def _():
        grad[...] += part

    @pl.when(j == pl.num_programs(0) - 1)
    def _():
        grad_b[...] = grad[...].astype(narrow)


def first_own(place, users, items, relation, targets, turn):
    n, d = users.shape
    m = items.shape[0]
    tile = pl.BlockSpec((TILE, d), lambda j, place: (j, 0))
    labels = pl.BlockSpec((None, n, TILE), lambda j, place: (turn, place[0], j))
    return call(
        first_body,
        (m // TILE,),
        [whole(n, d), tile, whole(d, d), labels],
        [
            tile,
            tile,
            whole(n, d),
            pl.BlockSpec((n, TILE), lambda j, place: (0, j)),
            whole(n, d),
        ],
        [
            shape(narrow, m, d),
            shape(narrow, m, d),
            shape(narrow, n, d),
            shape(narrow, n, m),
            shape(narrow, n, d),
        ],
        [pltpu.VMEM((n, d), single)],
        2 * n * d * d + 2 * m * d * d + 4 * n * m * d,
        prefetch=1,
    )(place, users, items, relation, targets)


def peer_body(
    place, sums, users, relation, items_b, targets, mapped, errors_o, anchor_o, table,
    users_b, errors_p, grad_b, items_next, sums_next,
    v_relation, v_items, v_labels, v_mapped, v_errors_o, v_anchor_o, v_table,
    v_anchor, v_errors, v_grad, v_next, v_sums, v_lines, sems,
    turn,
):
    go = Copies(sems)
    n = users.shape[0]
    get_relation = go.start(relation, v_relation)
    get_items = go.start(items_b, v_items)
    get_labels = []
    for at in tiles(n):
        rows = pl.ds(pl.multiple_of((1 - place[0]) * n + at.start, TILE), TILE)
        get_labels.append(go.start(targets.at[turn, rows], v_labels.at[at, :]))
    get_mapped = go.start(mapped, v_mapped)
    get_errors = go.start(errors_o, v_errors_o)
    get_anchor = go.start(anchor_o, v_anchor_o)
    get_table = go.start(table, v_table)
    go.send(users, users_b)
    columns_into(v_sums, sums[...])
    get_relation.wait()
    v_anchor[...] = dot(users[...], v_relation[...], 1, 0).astype(narrow)
    get_items.wait()
    for at, copy in zip(tiles(n), get_labels):
        copy.wait()
        scores = dot(v_anchor[at, :], v_items[...], 1, 1)
        v_errors[at, :] = errors_of(scores, v_labels[at, :])
    go.send(v_errors, errors_p)
    get_mapped.wait()
    v_grad[...] = dot(v_errors[...], v_mapped[...], 1, 0).astype(narrow)
    go.send(v_grad, grad_b)
    get_errors.wait()
    get_anchor.wait()
    get_table.wait()
    for at in tiles(v_items.shape[0]):
        grads = dot(v_errors_o[:, at], v_anchor_o[...], 0, 0) + dot(v_errors[:, at], v_anchor[...], 0, 0)
        new, accum = adagrad_rows(v_table[at, :], v_sums[at, :1], grads)
        v_next[at, :] = new.astype(narrow)
        v_lines[at, :] = jnp.broadcast_to(accum, (TILE, 128))
        go.send(v_next.at[at, :], items_next.at[at, :])
    for at in tiles(v_items.shape[0]):
        sums_next[:, at] = jnp.transpose(v_lines[at, :])[:1, :]
    go.finish()


def first_peer(place, users, relation, items_b, targets, mapped, errors_o, anchor_o, table, sums, turn):
    n, d = users.shape
    m = table.shape[0]
    line = pl.BlockSpec(memory_space=pltpu.VMEM)
    return manual(
        functools.partial(peer_body, turn=turn),
        [pl.BlockSpec(memory_space=pltpu.SMEM), line, line] + [anywhere()] * 7,
        [anywhere()] * 4 + [line],
        [
            shape(narrow, n, d),
            shape(narrow, n, m),
            shape(narrow, n, d),
            shape(narrow, m, d),
            shape(single, 1, m),
        ],
        [
            pltpu.VMEM((d, d), narrow),
            pltpu.VMEM((m, d), narrow),
            pltpu.VMEM((n, m), narrow),
            pltpu.VMEM((m, d), narrow),
            pltpu.VMEM((n, m), narrow),
            pltpu.VMEM((n, d), narrow),
            pltpu.VMEM((m, d), single),
            pltpu.VMEM((n, d), narrow),
            pltpu.VMEM((n, m), narrow),
            pltpu.VMEM((n, d), narrow),
            pltpu.VMEM((m, d), narrow),
            pltpu.VMEM((m, 8), single),
            pltpu.VMEM((m, 128), single),
        ],
        10 + n // TILE + m // TILE,
        2 * n * d * d + 8 * n * m * d,
    )(place, sums, users, relation, items_b, targets, mapped, errors_o, anchor_o, table)


def ahead_body(table, grad, more, sums, relation, turned, anchor):
    new, _ = adagrad_rows(wide(table[...]), as_column(sums[...]), wide(grad[...]) + wide(more[...]))
    new = new.astype(narrow)
    turned[...] = jnp.transpose(new)
    anchor[...] = dot(new, relation[...], 1, 0).astype(narrow)


def ahead(table, grad, more, sums, relation):
    n, d = table.shape
    tile = pl.BlockSpec((TILE, d), lambda j: (j, 0))
    return call(
        ahead_body,
        (n // TILE,),
        [tile, tile, tile, pl.BlockSpec((1, TILE), lambda j: (0, j)), whole(d, d)],
        [pl.BlockSpec((d, TILE), lambda j: (0, j)), tile],
        [shape(narrow, d, n), shape(narrow, n, d)],
        [],
        2 * n * d * d,
    )(table, grad, more, sums, relation)


def term_body(users_o, users_p, errors_o, errors_p, items, term, turned_o, turned_p):
    j = pl.program_id(0)

    @pl.when(j == 0)
    def _():
        turned_o[...] = jnp.transpose(users_o[...])
        turned_p[...] = jnp.transpose(users_p[...])

    crossed = dot(turned_o[...], errors_o[...], 1, 0) + dot(turned_p[...], errors_p[...], 1, 0)
    part = dot(crossed.astype(narrow), items[...], 1, 0)

    @pl.when(j == 0)
    def _():
        term[...] = part

    @pl.when(j > 0)
    def _():
        term[...] += part


def first_term(users_o, users_p, errors_o, errors_p, items):
    n, d = users_o.shape
    m = items.shape[0]
    tile = pl.BlockSpec((TILE, d), lambda j: (j, 0))
    side = pl.BlockSpec((n, TILE), lambda j: (0, j))
    return call(
        term_body,
        (m // TILE,),
        [whole(n, d), whole(n, d), side, side, tile],
        whole(d, d),
        shape(single, d, d),
        [pltpu.VMEM((d, n), narrow), pltpu.VMEM((d, n), narrow)],
        4 * n * m * d + 2 * m * d * d,
    )(users_o, users_p, errors_o, errors_p, items)


def second_body(
    place, sums, item_sums, table, grad, more, relation, anchor_p, turned_p, items, targets, term,
    users_next, errors, term_keep, term_give, next_a, next_b, sums_next, item_sums_next,
    v_table, v_grad, v_more, v_relation, v_anchor, v_turned, v_items, v_labels, v_term,
    v_users, v_errors, v_crossed, v_next, v_sums, v_lines, sems,
    turn,
):
    go = Copies(sems)
    n, d = table.shape
    m = items.shape[0]
    get_table = []
    for at in tiles(n):
        for source, target in ((more, v_more), (grad, v_grad), (table, v_table)):
            get_table.append(go.start(source.at[at, :], target.at[at, :]))
    get_relation = go.start(relation, v_relation)
    get_anchor = go.start(anchor_p, v_anchor.at[n:, :])
    get_items = go.start(items, v_items)
    get_labels = []
    for half, first in ((0, place[0]), (n, 1 - place[0])):
        for at in tiles(n):
            rows = pl.ds(pl.multiple_of(first * n + at.start, TILE), TILE)
            get_labels.append(
                go.start(targets.at[turn, rows], v_labels.at[half + at.start : half + at.stop, :])
            )
    get_turned = go.start(turned_p, v_turned.at[:, n:])
    get_term = go.start(term, v_term)
    columns_into(v_sums.at[:n, :], sums[...])
    columns_into(v_sums.at[n:, :], item_sums[...])
    for k, at in enumerate(tiles(n)):
        for copy in get_table[3 * k : 3 * k + 3]:
            copy.wait()
        new, accum = adagrad_rows(
            v_table[at, :], v_sums[at, :1], wide(v_grad[at, :]) + wide(v_more[at, :])
        )
        v_users[at, :] = new
        v_lines[at, :] = jnp.broadcast_to(accum, (TILE, 128))
        v_turned[:, at] = jnp.transpose(new.astype(narrow))
    go.send(v_users, users_next)
    get_relation.wait()
    v_anchor[:n, :] = dot(v_users[...].astype(narrow), v_relation[...], 1, 0).astype(narrow)
    get_items.wait()
    for at, copy in zip(tiles(2 * n), get_labels):
        if at.start == n:
            get_anchor.wait()
        copy.wait()
        scores = dot(v_anchor[at, :], v_items[...], 1, 1)
        v_errors[at, :] = errors_of(scores, v_labels[at, :])
        go.send(v_errors.at[at, :], errors.at[at, :])
    get_turned.wait()
    get_term.wait()
    for at in tiles(d):
        v_crossed[at, :] = dot(v_turned[at, :], v_errors[...], 1, 0).astype(narrow)
        v_term[at, :] += dot(v_crossed[at, :], v_items[...], 1, 0)
    half = d // 2
    keep = pl.multiple_of(place[1] * half, half)
    give = pl.multiple_of((1 - place[1]) * half, half)
    go.send(v_term.at[pl.ds(give, half), :], term_give)
    go.send(v_term.at[pl.ds(keep, half), :], term_keep)
    for at in tiles(m):
        grads = dot(v_errors[:, at], v_anchor[...], 0, 0)
        below = slice(n + at.start, n + at.stop)
        new, accum = adagrad_rows(wide(v_items[at, :]), v_sums[below, :1], grads)
        v_next[at, :] = new.astype(narrow)
        v_lines[below, :] = jnp.broadcast_to(accum, (TILE, 128))
        if at.start < m // 2:
            go.send(v_next.at[at, :], next_a.at[at, :])
        else:
            go.send(v_next.at[at, :], next_b.at[at.start - m // 2 : at.stop - m // 2, :])
    for at in tiles(n + m):
        line = jnp.transpose(v_lines[at, :])[:1, :]
        if at.start < n:
            sums_next[:, at] = line
        else:
            item_sums_next[:, at.start - n : at.stop - n] = line
    go.finish()


def second(place, table, grad, more, sums, relation, anchor_p, turned_p, items, item_sums, targets, term, turn):
    n, d = table.shape
    m = items.shape[0]
    line = pl.BlockSpec(memory_space=pltpu.VMEM)
    return manual(
        functools.partial(second_body, turn=turn),
        [pl.BlockSpec(memory_space=pltpu.SMEM), line, line] + [anywhere()] * 9,
        [anywhere()] * 6 + [line, line],
        [
            shape(single, n, d),
            shape(narrow, 2 * n, m),
            shape(single, d // 2, d),
            shape(single, d // 2, d),
            shape(narrow, m // 2, d),
            shape(narrow, m // 2, d),
            shape(single, 1, n),
            shape(single, 1, m),
        ],
        [
            pltpu.VMEM((n, d), single),
            pltpu.VMEM((n, d), narrow),
            pltpu.VMEM((n, d), narrow),
            pltpu.VMEM((d, d), narrow),
            pltpu.VMEM((2 * n, d), narrow),
            pltpu.VMEM((d, 2 * n), narrow),
            pltpu.VMEM((m, d), narrow),
            pltpu.VMEM((2 * n, m), narrow),
            pltpu.VMEM((d, d), single),
            pltpu.VMEM((n, d), single),
            pltpu.VMEM((2 * n, m), narrow),
            pltpu.VMEM((d, m), narrow),
            pltpu.VMEM((m, d), narrow),
            pltpu.VMEM((n + m, 8), single),
            pltpu.VMEM((n + m, 128), single),
        ],
        9 + 7 * (n // TILE) + m // TILE,
        2 * n * d * d + 12 * n * m * d + 2 * m * d * d,
    )(place, sums, item_sums, table, grad, more, relation, anchor_p, turned_p, items, targets, term)


def grads_body(errors, items, relation, grad_o, grad_p,
               v_errors, v_items, v_relation, v_mapped, v_grad_o, v_grad_p, sems):
    go = Copies(sems)
    n = grad_o.shape[0]
    get_items = go.start(items, v_items)
    get_relation = go.start(relation, v_relation)
    rows = tiles(2 * n)
    order = rows[len(rows) // 2 :] + rows[: len(rows) // 2]
    get = [go.start(errors.at[at, :], v_errors.at[at, :]) for at in order]
    get_items.wait()
    get_relation.wait()
    v_mapped[...] = dot(v_items[...], v_relation[...], 1, 1).astype(narrow)
    for at, copy in zip(order, get):
        copy.wait()
        part = dot(v_errors[at, :], v_mapped[...], 1, 0)
        if at.start >= n:
            there = slice(at.start - n, at.stop - n)
            v_grad_p[there, :] = part.astype(narrow)
            go.send(v_grad_p.at[there, :], grad_p.at[there, :])
        else:
            v_grad_o[at, :] = part
            go.send(v_grad_o.at[at, :], grad_o.at[at, :])
    go.finish()


def second_grads(errors, items, relation):
    n = errors.shape[0] // 2
    m, d = items.shape
    return manual(
        grads_body,
        [anywhere()] * 3,
        [anywhere()] * 2,
        [shape(single, n, d), shape(narrow, n, d)],
        [
            pltpu.VMEM((2 * n, m), narrow),
            pltpu.VMEM((m, d), narrow),
            pltpu.VMEM((d, d), narrow),
            pltpu.VMEM((m, d), narrow),
            pltpu.VMEM((n, d), single),
            pltpu.VMEM((n, d), narrow),
        ],
        2 + 4 * (n // TILE),
        4 * n * m * d + 2 * m * d * d,
    )(errors, items, relation)


def users_body(table, grad, more, sums, table_next, sums_next):
    new, accum = adagrad_rows(table[...], as_column(sums[...]), grad[...] + wide(more[...]))
    table_next[...] = new
    sums_next[...] = as_line(accum)


def update_users(table, grad, more, sums):
    n, d = table.shape
    tile = pl.BlockSpec((TILE, d), lambda j: (j, 0))
    line = pl.BlockSpec((1, TILE), lambda j: (0, j))
    return call(
        users_body,
        (n // TILE,),
        [tile, tile, tile, line],
        [tile, line],
        [shape(single, n, d), shape(single, 1, n)],
        [],
        4 * n * d,
        limit=16,
    )(table, grad, more, sums)


def final_body(place, mine, other, sums, step, sums_next, *, count):
    half = mine.shape[0]
    for part, side in ((mine, place[1]), (other, 1 - place[1])):
        rows = pl.ds(pl.multiple_of(side * half, half), half)
        grads = wide(part[...]) / count
        _, accum = adagrad_rows(grads, as_column(sums[:, rows]), grads)
        step[rows, :] = grads * lax.rsqrt(accum + epsilon)
        sums_next[:, rows] = as_line(accum)


def final(place, mine, other, sums, count):
    d = mine.shape[1]
    whole_array = pl.BlockSpec(memory_space=pltpu.VMEM)
    return pl.pallas_call(
        functools.partial(final_body, count=count),
        name="final",
        in_specs=[pl.BlockSpec(memory_space=pltpu.SMEM)] + [whole_array] * 3,
        out_specs=[whole_array] * 2,
        out_shape=[shape(single, d, d), shape(single, 1, d)],
        compiler_params=pltpu.CompilerParams(vmem_limit_bytes=16 << 20),
    )(place, mine, other, sums)


def pick(parts, key):
    n = len(parts)
    level = 1
    while level < n:
        bit = (key // level) % 2 == 1
        parts = [jnp.where(bit, parts[k ^ level], parts[k]) for k in range(n)]
        level *= 2
    return jnp.concatenate(parts, axis=0)


def relation_total(keep, give):
    blocks = lax.axis_size("blk")
    b, r = lax.axis_index("blk"), lax.axis_index("rel")
    half = keep.shape[0]
    p = keep + exchange(give, 1, 0)
    key = r + 2 * ((b // 2) % 2)
    part = half // 4
    total = lax.dynamic_slice_in_dim(p, key * part, part)
    got = []
    for k in (3, 1, 2):
        piece = lax.dynamic_slice_in_dim(p, (key ^ k) * part, part).astype(narrow)
        got.append(wide(exchange(piece, 2 * (k // 2), k % 2)))
    total = total + (got[0] + (got[1] + got[2]))
    flip = 4
    while blocks // flip > 8:
        sent = total.astype(narrow)
        total = wide(sent) + wide(exchange(sent, flip, 0))
        flip *= 2
    sent = total.astype(narrow)
    parts = [wide(sent)]
    for k in range(1, blocks // flip):
        parts.append(wide(exchange(sent, flip * k, 0)))
    while len(parts) > 1:
        parts = [parts[i] + parts[i + 1] for i in range(0, len(parts), 2)]
    sent = parts[0].astype(narrow)
    parts = [sent] + [exchange(sent, 2 * (k // 2), k % 2) for k in (1, 2, 3)]
    p = pick(parts, key)
    return p, exchange(p, 1, 0)


def step(user_table, user_accum, item_table, item_accum, relation, relation_accum, targets):
    blocks = lax.axis_size("blk")
    rounds = targets.shape[0]
    assert rounds == 2 and lax.axis_size("rel") == 2
    place = jnp.stack([lax.axis_index("rel"), lax.axis_index("blk") % 2]).astype(jnp.int32)
    sums_o, item_sums = user_accum[None, :], item_accum[None, :]

    mine = user_table.astype(narrow)
    theirs = swap(mine)
    items, mapped, anchor_o, errors_o, grad_ob = first_own(
        place[:1], mine, item_table, relation, targets, 0
    )
    more_p = swap(grad_ob)
    sums_p = swap(sums_o)
    users_p, errors_p, grad_pb, items_next, item_sums = first_peer(
        place, theirs, relation, items, targets, mapped, errors_o, anchor_o, item_table, item_sums, 0
    )
    more_o = swap(grad_pb)
    items_next = from_behind(items_next)
    item_sums = from_behind(item_sums)
    term = first_term(mine, users_p, errors_o, errors_p, items)
    turned_p, anchor_p = ahead(users_p, grad_pb, more_p, sums_p, relation)

    users, errors, keep, give, *chunks, sums_o, item_sums = second(
        place, user_table, grad_ob, more_o, sums_o, relation, anchor_p, turned_p,
        items_next, item_sums, targets, term, 1,
    )
    grad_o, grad_pb = second_grads(errors, items_next, relation)
    more_o = swap(grad_pb)
    chunks = [from_behind(chunk) for chunk in chunks]
    item_sums = from_behind(item_sums)
    users, sums_o = update_users(users, grad_o, more_o, sums_o)

    relation_step, accum_next = final(
        place, *relation_total(keep, give), relation_accum[None, :], blocks * rounds
    )
    items_last = jnp.concatenate([wide(chunk) for chunk in chunks], axis=0)
    item_sums = jnp.maximum(item_sums[0], 0.0)
    return (users, sums_o[0], items_last, item_sums, relation_step, accum_next[0])


def solution(mesh):
    rows = P(("blk", "rel"), None)
    line = P(("blk", "rel"))
    return jax.shard_map(
        step,
        mesh=mesh,
        in_specs=(rows, line, rows, line, P(), P(), P(None, "blk", "rel")),
        out_specs=(rows, line, rows, line, P(), P()),
        check_vma=False,
    )
```
